32 devices in a mesh: gx: 8 (over z, y), gy: 4 (over x, core).
Axes of the slice: x: 2, y: 2, z: 4, core: 2. Of those that a mesh axis runs over, the one named last changes fastest.
Arguments:
- populations: float32 [19, 64, 256, 128], P(None, 'gx', 'gy'), may hold values from 0.5 to 2
- solid_flags: int32 [64, 256, 128], P('gx', 'gy'), may hold values 0 or 1
- point_cells: int32 [3, 4608], replicated, may hold values from 0 to 255, as said below
- point_turbine: int32 [4608], replicated, may hold values from 0 to 23, as said below
- blade_speed: float32 [3, 4608], replicated, may hold values from -0.3 to 0.3
- chord: float32 [4608], replicated, may hold values from 0.3 to 3
- turbine_gain: float32 [24], replicated, may hold values from 0.5 to 2
Outputs:
- read: float32 [19, 64, 256, 128], P(None, 'gx', 'gy')
- point_force: float32 [3, 4608], replicated
The draws below stay inside these ranges and needn't reach their ends.
Inputs may be any that keep to these rules, and one draw needn't show every extreme that they name: `point_cells`: row 0 and row 1 are a point's streamwise and spanwise cell, row 2 its height, which lies in [4, 124]; all points of one turbine share the streamwise cell. `point_turbine`: each turbine has exactly 192 points.
All inputs are finite; a program needn't handle non-finite values. No bound on the sum of `solid_flags` on one device may be relied on, other than what follows from the above.
Results may differ from the reference program's by a relative error of at most 0.00007.
Values sent between devices are 32-bit elements; how exact they have to be, the bound alone decides.
A program may use at most 128 MiB of HBM per device.

```python
import math
import jax
import jax.numpy as jnp
from jax import lax

CX = 8
CY = 64
NZ = 128
TURB = 24
BLADES = 3
BLADE_PTS = 64
SMEAR = 3
POINTS = 4608
NX = 64
NY = 256


def place_points(key):
    base = jax.random.fold_in(key, 11)
    keys = jax.random.split(base, 5)
    hub_x = jax.random.randint(keys[0], (TURB,), 0, NX, dtype=jnp.int32)
    hub_y = jax.random.randint(keys[1], (TURB,), 0, NY, dtype=jnp.int32)
    within_x = jax.random.randint(jax.random.fold_in(base, 21), (2,), 0, CX, dtype=jnp.int32)
    within_y = jax.random.randint(jax.random.fold_in(base, 22), (2,), 0, CY, dtype=jnp.int32)
    hub_x = hub_x.at[0].set(NX // 2 + within_x[0]).at[1].set(within_x[1])
    hub_y = hub_y.at[0].set(within_y[0]).at[1].set(within_y[1])
    owner = jax.random.permutation(keys[2], jnp.repeat(jnp.arange(TURB, dtype=jnp.int32), BLADES * BLADE_PTS))
    reach = NZ // 2 - SMEAR - 1
    off_y = jax.random.randint(keys[3], (POINTS,), -reach, reach + 1, dtype=jnp.int32)
    off_z = jax.random.randint(keys[4], (POINTS,), -reach, reach + 1, dtype=jnp.int32)
    pos_x = hub_x[owner]
    pos_y = (hub_y[owner] + off_y) % NY
    pos_z = NZ // 2 + off_z
    return (jnp.stack([pos_x, pos_y, pos_z], axis=0).astype(jnp.int32), owner.astype(jnp.int32))


def draw_point_cells(key, part):
    return place_points(key)[0]


def draw_point_turbine(key, part):
    return place_points(key)[1]


def set_ends(values, own_key, low, top_value):
    dims = values.shape
    index_at = [jax.random.randint(jax.random.fold_in(own_key, axis), (), 0, dims[axis]) for axis in range(len(dims))]
    values = values.at[tuple(index_at)].set(low)
    longest = dims.index(max(dims))
    index_at[longest] = (index_at[longest] + 1) % dims[longest]
    return values.at[tuple(index_at)].set(top_value)


def block_levels(rng, shape, shards, smallest, top_value):
    loudness = 1.0
    for dim, parts in shards:
        draws = jax.random.uniform(jax.random.fold_in(jax.random.fold_in(rng, 6), dim), (parts,), jnp.float32, smallest / len(shards), top_value / len(shards))
        loudness = loudness * jnp.repeat(jnp.exp(draws), shape[dim] // parts).reshape((-1,) + (1,) * (len(shape) - 1 - dim))
    return loudness


def gaussian(key, extent, scale, most, held_as=jnp.bfloat16):
    return jnp.clip(scale * jax.random.normal(key, extent, jnp.float32), -most, most).astype(held_as)


def setup_inputs(seed: int = 0) -> dict:
    arg_keys = jax.random.split(jax.random.key(seed), 8)
    populations = jnp.clip(jnp.exp(math.log(2.0) - 1.3862944 * jax.random.uniform(arg_keys[0], (19, NX, NY, NZ), jnp.float32) ** block_levels(arg_keys[0], (19, NX, NY, NZ), ((1, 8), (2, 4)), -0.2, 0.2)), 0.5, 2.0)
    solid_flags = set_ends((jax.random.randint(arg_keys[1], (NX, NY, NZ), 0, 16) < 1).astype(jnp.int32), jax.random.fold_in(arg_keys[1], 1), 0, 1)
    point_cells = draw_point_cells(jax.random.fold_in(arg_keys[7], 71), 0)
    point_turbine = draw_point_turbine(jax.random.fold_in(arg_keys[7], 71), 0)
    blade_speed = gaussian(arg_keys[4], (3, POINTS), 0.05, 0.3, jnp.float32)
    chord = jnp.clip(jnp.exp(jax.random.uniform(arg_keys[5], (POINTS,), jnp.float32, math.log(0.3), math.log(3.0))), 0.3, 3.0)
    turbine_gain = jnp.clip(jnp.exp(jax.random.uniform(arg_keys[6], (TURB,), jnp.float32, math.log(0.5), math.log(2.0))), 0.5, 2.0)
    return {"populations": populations, "solid_flags": solid_flags, "point_cells": point_cells, "point_turbine": point_turbine, "blade_speed": blade_speed, "chord": chord, "turbine_gain": turbine_gain}


lattice_dirs = [(0, 0, 0), (1, 0, 0), (-1, 0, 0), (0, 1, 0), (0, -1, 0), (0, 0, 1), (0, 0, -1), (1, 1, 0), (-1, -1, 0), (1, -1, 0), (-1, 1, 0), (1, 0, 1), (-1, 0, -1), (1, 0, -1), (-1, 0, 1), (0, 1, 1), (0, -1, -1), (0, 1, -1), (0, -1, 1)]
opposite_dir = [0, 2, 1, 4, 3, 6, 5, 8, 7, 10, 9, 12, 11, 14, 13, 16, 15, 18, 17]
lattice_wts = [1.0 / 3.0] + [1.0 / 18.0] * 6 + [1.0 / 36.0] * 12
relax_time = 0.8
kernel_scale = 1.5
high = lax.Precision.HIGHEST

def kernel_value(offset):
    dist = offset.astype(jnp.float32)
    return jnp.where(jnp.abs(offset) <= SMEAR, jnp.exp(-(dist / kernel_scale) ** 2), jnp.float32(0.0))

def collide(pops, rho, mom, force, solid_flags):
    cvec = jnp.array(lattice_dirs, jnp.float32).T
    vel = (mom + 0.5 * force) / rho
    cu = jnp.einsum('ci,cxyz->ixyz', cvec, vel, precision=high)
    cf = jnp.einsum('ci,cxyz->ixyz', cvec, force, precision=high)
    usq = lax.optimization_barrier(jnp.sum(vel * vel, axis=0))
    uf = lax.optimization_barrier(jnp.sum(vel * force, axis=0))
    geq = rho * (1.0 + 3.0 * cu + 4.5 * cu * cu - 1.5 * usq)
    source = (1.0 - 0.5 / relax_time) * (3.0 * (cf - uf) + 9.0 * cu * cf)
    post = pops - (pops - geq) / relax_time + source
    bounce = pops[jnp.array(opposite_dir, jnp.int32)]
    return jnp.where(solid_flags[None] != 0, bounce, post)

def reference(populations, solid_flags, point_cells, point_turbine, blade_speed, chord, turbine_gain):
    wts = jnp.array(lattice_wts, jnp.float32)
    cvec = jnp.array(lattice_dirs, jnp.float32).T
    rho = jnp.einsum('i,ixyz->xyz', wts, populations, precision=high)
    mom = jnp.einsum('ci,ixyz->cxyz', cvec * wts[None], populations, precision=high)
    vel_raw = mom / rho[None]
    pos_x, pos_y, pos_z = (point_cells[0], point_cells[1], point_cells[2])
    sampled = vel_raw[:, pos_x, pos_y, pos_z]
    rel = sampled - blade_speed
    coef = chord * turbine_gain[point_turbine]
    speed = jnp.sqrt(lax.optimization_barrier(jnp.sum(rel * rel, axis=0)) + 0.0001)
    point_force = -(coef * speed)[None] * rel
    span = jnp.arange(-SMEAR, SMEAR + 1, dtype=jnp.int32)
    off_x, off_y, off_z = jnp.meshgrid(span, span, span, indexing='ij')
    off_x, off_y, off_z = (off_x.reshape(-1), off_y.reshape(-1), off_z.reshape(-1))
    kern = kernel_value(off_x) * kernel_value(off_y) * kernel_value(off_z)
    cell_x = (pos_x[:, None] + off_x[None]) % NX
    cell_y = (pos_y[:, None] + off_y[None]) % NY
    cell_z = pos_z[:, None] + off_z[None]
    values = point_force[:, :, None] * kern[None, None]
    force = jnp.zeros((3, NX, NY, NZ), jnp.float32).at[:, cell_x, cell_y, cell_z].add(values)
    post = collide(populations, rho[None], mom, force, solid_flags)
    outs = []
    for index in range(19):
        step_x, step_y, step_z = lattice_dirs[index]
        moved = jnp.roll(post[index], (step_x, step_y), axis=(0, 1))
        mirror = post[opposite_dir[index]]
        if step_z == 1:
            moved = jnp.concatenate([mirror[:, :, :1], moved[:, :, :-1]], axis=2)
        elif step_z == -1:
            moved = jnp.concatenate([moved[:, :, 1:], mirror[:, :, -1:]], axis=2)
        outs.append(moved)
    return (jnp.stack(outs, axis=0), point_force)
```

```python
import functools
import math

import jax
import jax.numpy as jnp
import numpy as np
from jax import lax
from jax.experimental import pallas as pl
from jax.experimental.pallas import tpu as pltpu
from jax.sharding import PartitionSpec as P

SMEAR = 3
lattice_dirs = [
    (0, 0, 0),
    (1, 0, 0),
    (-1, 0, 0),
    (0, 1, 0),
    (0, -1, 0),
    (0, 0, 1),
    (0, 0, -1),
    (1, 1, 0),
    (-1, -1, 0),
    (1, -1, 0),
    (-1, 1, 0),
    (1, 0, 1),
    (-1, 0, -1),
    (1, 0, -1),
    (-1, 0, 1),
    (0, 1, 1),
    (0, -1, -1),
    (0, 1, -1),
    (0, -1, 1),
]
opposite_dir = [0, 2, 1, 4, 3, 6, 5, 8, 7, 10, 9, 12, 11, 14, 13, 16, 15, 18, 17]
lattice_wts = [1.0 / 3.0] + [1.0 / 18.0] * 6 + [1.0 / 36.0] * 12
relax_time = 0.8
kernel_scale = 1.5
NDIR = 19
EAST = [k for k in range(NDIR) if lattice_dirs[k][0] == 1]
WEST = [k for k in range(NDIR) if lattice_dirs[k][0] == -1]
NORTH = [k for k in range(NDIR) if lattice_dirs[k][1] == 1]
SOUTH = [k for k in range(NDIR) if lattice_dirs[k][1] == -1]
CORNERS = [7, 8, 9, 10]
MESH = pl.DeviceIdType.MESH
f32 = jnp.float32
bf16 = jnp.bfloat16
NT = (((1,), (1,)), ((), ()))
VLIM = 48 * 1024 * 1024
SORT_CHUNK = 512


def split3(x):
    a = x.astype(bf16).astype(f32)
    r = x - a
    b = r.astype(bf16).astype(f32)
    return a, b, r - b


def iota(shape, dim):
    return lax.broadcasted_iota(jnp.int32, shape, dim)


def moments(g):
    side = g[1]
    for k in range(2, 7):
        side = side + g[k]
    diag = g[7]
    for k in range(8, 19):
        diag = diag + g[k]
    rho = g[0] * (1.0 / 3.0) + side * (1.0 / 18.0) + diag * (1.0 / 36.0)
    mom = []
    for axis in range(3):
        first, rest = None, None
        for k in range(1, 19, 2):
            step = lattice_dirs[k][axis]
            if step == 0:
                continue
            diff = g[k] - g[k + 1] if step == 1 else g[k + 1] - g[k]
            if k < 7:
                first = diff if first is None else first + diff
            else:
                rest = diff if rest is None else rest + diff
        mom.append(first * (1.0 / 18.0) + rest * (1.0 / 36.0))
    return rho, mom


def sample_kernel(
    turbines,
    hub_ref,
    cells_ref,
    turb_ref,
    blade_ref,
    chord_ref,
    gain_ref,
    pops_hbm,
    samp_ref,
    table_ref,
    rank_ref,
    pops,
    acc_ref,
    sems,
):
    wx, wy, nz = pops.shape[1:]
    points = turb_ref.shape[1]
    group = points // turbines
    start_x = lax.axis_index("gx") * wx
    start_y = lax.axis_index("gy") * wy

    def plane_copy(x):
        return pltpu.make_async_copy(pops_hbm.at[:, x], pops.at[:, x], sems.at[x])

    for x in range(wx):
        plane_copy(x).start()

    lanes = 128
    chunks = points // lanes
    hot = []
    for k in range(chunks):
        own = turb_ref[:, k * lanes : (k + 1) * lanes]
        hot.append((own == iota((turbines, lanes), 0)).astype(f32))
    stacked = jnp.concatenate(hot, axis=0).astype(bf16)
    upto = (iota((lanes, lanes), 0) <= iota((lanes, lanes), 1)).astype(bf16)
    inside = jnp.dot(stacked, upto, preferred_element_type=f32)
    whole = jnp.dot(stacked, jnp.ones((lanes, lanes), bf16), preferred_element_type=f32)
    before = jnp.full((turbines, lanes), -1.0, f32)
    for k in range(chunks):
        rows = slice(k * turbines, (k + 1) * turbines)
        rank = jnp.sum(hot[k] * (inside[rows] + before), axis=0, keepdims=True)
        rank_ref[:, k * lanes : (k + 1) * lanes] = rank
        before = before + whole[rows]

    acc_ref[...] = jnp.zeros_like(acc_ref)

    def sort_chunk(k, carry):
        cols = pl.ds(pl.multiple_of(k * SORT_CHUNK, SORT_CHUNK), SORT_CHUNK)
        mine = turb_ref[:, cols] == iota((turbines, SORT_CHUNK), 0)
        pos_y = cells_ref[1:2, cols].astype(f32)
        pos_z = cells_ref[2:3, cols].astype(f32)
        y_high = pos_y.astype(bf16).astype(f32)
        rows = [y_high, pos_y - y_high, pos_z]
        for c in range(3):
            rows += list(split3(blade_ref[c : c + 1, cols]))
        rows += list(split3(chord_ref[:, cols] * gain_ref[...]))
        data = jnp.concatenate([jnp.where(mine, r, 0.0) for r in rows], axis=0).astype(bf16)
        place = (rank_ref[:, cols] == iota((group, SORT_CHUNK), 0).astype(f32)).astype(f32)
        acc_ref[...] += lax.dot_general(
            data, place.astype(bf16), NT, preferred_element_type=f32
        )
        return carry

    lax.fori_loop(0, points // SORT_CHUNK, sort_chunk, 0)

    def part(j):
        return acc_ref[j * turbines : (j + 1) * turbines]

    table_ref[0:turbines] = part(0) + part(1)
    table_ref[turbines : 2 * turbines] = part(2)
    for q in range(4):
        at = 3 + 3 * q
        table_ref[(2 + q) * turbines : (3 + q) * turbines] = part(at) + part(at + 1) + part(at + 2)

    samp_ref[...] = jnp.zeros_like(samp_ref)
    for x in range(wx):
        plane_copy(x).wait()
    per = samp_ref.shape[1]

    def one_turbine(t, carry):
        lx = hub_ref[t] - start_x

        @pl.when((lx >= 0) & (lx < wx))
        def _():
            rho, mom = moments([pops[i, lx] for i in range(NDIR)])
            vel = jnp.concatenate([m / rho for m in mom], axis=0)
            split = jnp.concatenate(split3(vel), axis=0).astype(bf16)
            pos_y = table_ref[pl.ds(t, 1), :].astype(jnp.int32)
            pos_z = table_ref[pl.ds(turbines + t, 1), :].astype(jnp.int32)
            pick_z = (iota((nz, group), 0) == pos_z).astype(f32).astype(bf16)
            at_z = jnp.dot(split, pick_z, preferred_element_type=f32)
            n = 3 * wy
            at_z = at_z[:n] + at_z[n : 2 * n] + at_z[2 * n :]
            pick_y = iota((wy, group), 0) + start_y == pos_y
            for c in range(3):
                one = jnp.sum(
                    jnp.where(pick_y, at_z[c * wy : (c + 1) * wy], 0.0), axis=0, keepdims=True
                )
                row = c * turbines + t
                samp_ref[row // per, pl.ds(row % per, 1), :] = one

        return carry

    lax.fori_loop(0, turbines, one_turbine, 0)


def reduce_kernel(nx, ny, s_ref, out_ref, rx, ry, red, ss1, sr1, ss2, sr2, ss3, sr3):
    gx = lax.axis_index("gx")
    gy = lax.axis_index("gy")
    xs = [lax.rem(gx + k, nx) for k in range(nx)]
    ys = [lax.rem(gy + k, ny) for k in range(ny)]
    barrier = pltpu.get_barrier_semaphore()
    for k in range(1, nx):
        pl.semaphore_signal(barrier, inc=1, device_id=(xs[k], gy), device_id_type=MESH)
    for k in range(1, ny):
        pl.semaphore_signal(barrier, inc=1, device_id=(gx, ys[k]), device_id_type=MESH)
    pl.semaphore_wait(barrier, nx + ny - 2)

    first = []
    for k in range(1, nx):
        first.append(
            pltpu.make_async_remote_copy(
                src_ref=s_ref.at[xs[k]],
                dst_ref=rx.at[k],
                send_sem=ss1.at[k],
                recv_sem=sr1.at[k],
                device_id=(xs[k], gy),
                device_id_type=MESH,
            )
        )
        first[-1].start()
    total = s_ref[gx]
    for k in range(1, nx):
        first[k - 1].wait_recv()
        total = total + rx[k]
    red[...] = total

    second = []
    for k in range(1, ny):
        second.append(
            pltpu.make_async_remote_copy(
                src_ref=red,
                dst_ref=ry.at[k],
                send_sem=ss2.at[k],
                recv_sem=sr2.at[k],
                device_id=(gx, ys[k]),
                device_id_type=MESH,
            )
        )
        second[-1].start()
    for k in range(1, ny):
        second[k - 1].wait_recv()
        total = total + ry[k]
    out_ref[gx] = total

    third = []
    for k in range(1, nx):
        third.append(
            pltpu.make_async_remote_copy(
                src_ref=out_ref.at[gx],
                dst_ref=out_ref.at[gx],
                send_sem=ss3.at[k],
                recv_sem=sr3.at[k],
                device_id=(xs[k], gy),
                device_id_type=MESH,
            )
        )
        third[-1].start()
    for copy in first + second:
        copy.wait_send()
    for copy in third:
        copy.wait()


def wrapped(offset, total):
    offset = jnp.where(offset >= total // 2, offset - total, offset)
    return jnp.where(offset < -(total // 2), offset + total, offset)


def kernel_value(offset):
    dist = offset.astype(f32)
    return jnp.where(
        jnp.abs(offset) <= SMEAR, jnp.exp(-((dist / kernel_scale) ** 2)), jnp.float32(0.0)
    )


def collide_kernel(
    turbines,
    total_x,
    total_y,
    hub_ref,
    samp_ref,
    table_ref,
    solid_hbm,
    pops_hbm,
    pfs_ref,
    north_ref,
    south_ref,
    post_hbm,
    pops,
    solid,
    force,
    field,
    sems,
    out_sems,
):
    wx, wy, nz = pops.shape[1:]
    group = table_ref.shape[1]
    start_x = lax.axis_index("gx") * wx
    start_y = lax.axis_index("gy") * wy

    def plane_copy(x):
        return pltpu.make_async_copy(pops_hbm.at[:, x], pops.at[:, x], sems.at[x])

    def plane_out(x):
        return pltpu.make_async_copy(pops.at[:, x], post_hbm.at[:, x], out_sems.at[x])

    solid_copy = pltpu.make_async_copy(solid_hbm, solid, sems.at[wx])
    solid_copy.start()
    for x in range(wx):
        plane_copy(x).start()

    def rows(j):
        return table_ref[j * turbines : (j + 1) * turbines]

    rel = [samp_ref[c * turbines : (c + 1) * turbines] - rows(2 + c) for c in range(3)]
    speed = jnp.sqrt(rel[0] * rel[0] + rel[1] * rel[1] + rel[2] * rel[2] + 0.0001)
    scale = -(rows(5) * speed)
    for c in range(3):
        pfs_ref[c * turbines : (c + 1) * turbines] = scale * rel[c]

    force[...] = jnp.zeros_like(force)
    reach = [float(np.float32(math.exp(-((d / kernel_scale) ** 2)))) for d in range(SMEAR + 1)]

    def one_turbine(t, carry):
        hub = hub_ref[t]

        @pl.when(lax.rem(hub - start_x + SMEAR + total_x, total_x) < wx + 2 * SMEAR)
        def _():
            pos_y = table_ref[pl.ds(t, 1), :].astype(jnp.int32)
            pos_z = table_ref[pl.ds(turbines + t, 1), :].astype(jnp.int32)
            kern_y = kernel_value(wrapped(iota((wy, group), 0) + start_y - pos_y, total_y))
            kern_z = kernel_value(iota((nz, group), 0) - pos_z)
            left = jnp.concatenate(
                [kern_y * pfs_ref[pl.ds(c * turbines + t, 1), :] for c in range(3)], axis=0
            )
            field[...] = lax.dot_general(
                left, kern_z, NT, preferred_element_type=f32, precision=lax.Precision.HIGHEST
            )

            def one_plane(x, inner):
                away = jnp.abs(wrapped(start_x + x - hub, total_x))

                @pl.when(away <= SMEAR)
                def _():
                    kern_x = jnp.float32(reach[3])
                    for d in range(3):
                        kern_x = jnp.where(away == d, jnp.float32(reach[d]), kern_x)
                    for c in range(3):
                        force[c, x] += kern_x * field[c * wy : (c + 1) * wy]

                return inner

            lax.fori_loop(0, wx, one_plane, 0)

        return carry

    lax.fori_loop(0, turbines, one_turbine, 0)
    solid_copy.wait()
    step = 8

    def one_block(x, b):
        at = pl.ds(pl.multiple_of(b * step, step), step)
        g = [pops[i, x, at, :] for i in range(NDIR)]
        rho, mom = moments(g)
        frc = [force[c, x, at, :] for c in range(3)]
        inv = 1.0 / rho
        vel = [(mom[c] + 0.5 * frc[c]) * inv for c in range(3)]
        wall = solid[x, at, :] != 0
        usq = vel[0] * vel[0] + vel[1] * vel[1] + vel[2] * vel[2]
        uf = vel[0] * frc[0] + vel[1] * frc[1] + vel[2] * frc[2]
        om = 1.0 / relax_time
        pre = 1.0 - 0.5 / relax_time
        keep = 1.0 - om
        base = (om * rho) * (1.0 - 1.5 * usq) - (3.0 * pre) * uf
        quad = (4.5 * om) * rho
        lin = (3.0 * om) * rho
        pops[0, x, at, :] = jnp.where(wall, g[0], keep * g[0] + base)
        for k in range(1, NDIR, 2):
            cu, cf = None, None
            for axis in range(3):
                s = lattice_dirs[k][axis]
                if s == 0:
                    continue
                if cu is None:
                    cu, cf = (vel[axis], frc[axis]) if s == 1 else (-vel[axis], -frc[axis])
                elif s == 1:
                    cu, cf = cu + vel[axis], cf + frc[axis]
                else:
                    cu, cf = cu - vel[axis], cf - frc[axis]
            even = base + cu * (quad * cu + (9.0 * pre) * cf)
            odd = lin * cu + (3.0 * pre) * cf
            pops[k, x, at, :] = jnp.where(wall, g[k + 1], keep * g[k] + (even + odd))
            pops[k + 1, x, at, :] = jnp.where(wall, g[k], keep * g[k + 1] + (even - odd))

    def one_plane(x, carry):
        plane_copy(x).wait()

        def blocks(b, inner):
            one_block(x, b)
            return inner

        lax.fori_loop(0, wy // step, blocks, 0)
        for j, k in enumerate(NORTH):
            north_ref[j, pl.ds(x, 1), :] = pops[k, x, wy - 1 : wy, :]
        for j, k in enumerate(SOUTH):
            south_ref[j, pl.ds(x, 1), :] = pops[k, x, 0:1, :]

        @pl.when(x > 0)
        def _():
            plane_out(x - 1).start()

        return carry

    lax.fori_loop(0, wx, one_plane, 0)
    plane_out(wx - 1).start()
    for x in range(wx):
        plane_out(x).wait()


def halo_kernel(
    nx, ny, wx, post, north, south, from_w, from_e, from_s, from_n, from_c, send, recv
):
    gx = lax.axis_index("gx")
    gy = lax.axis_index("gy")
    east, west = lax.rem(gx + 1, nx), lax.rem(gx + nx - 1, nx)
    up, down = lax.rem(gy + 1, ny), lax.rem(gy + ny - 1, ny)
    barrier = pltpu.get_barrier_semaphore()
    near = [
        (east, gy), (west, gy), (gx, up), (gx, down),
        (east, up), (west, down), (east, down), (west, up),
    ]
    for dev in near:
        pl.semaphore_signal(barrier, inc=1, device_id=dev, device_id_type=MESH)
    pl.semaphore_wait(barrier, len(near))
    moves = []
    for j, k in enumerate(EAST):
        moves.append((post.at[k, wx - 1], from_w.at[j], (east, gy)))
    for j, k in enumerate(WEST):
        moves.append((post.at[k, 0], from_e.at[j], (west, gy)))
    moves.append((north, from_s, (gx, up)))
    moves.append((south, from_n, (gx, down)))
    for j, k in enumerate(CORNERS):
        side = north if k in NORTH else south
        ids = NORTH if k in NORTH else SOUTH
        moves.append((side.at[ids.index(k)], from_c.at[j], near[4 + j]))
    copies = []
    for n, (src, dst, dev) in enumerate(moves):
        copies.append(
            pltpu.make_async_remote_copy(
                src_ref=src,
                dst_ref=dst,
                send_sem=send.at[n],
                recv_sem=recv.at[n],
                device_id=dev,
                device_id_type=MESH,
            )
        )
        copies[-1].start()
    for copy in copies:
        copy.wait()


def stream_kernel(
    post_hbm, from_w, from_e, from_s, from_n, from_c, out_hbm, held, rows, outs, sems, out_sems
):
    wx = post_hbm.shape[1]
    wy, nz = post_hbm.shape[2:]

    def plane_in(x):
        return pltpu.make_async_copy(post_hbm.at[:, x], held.at[:, x + 1], sems.at[x])

    def plane_out(x):
        return pltpu.make_async_copy(outs.at[:, x], out_hbm.at[:, x], out_sems.at[x])

    for x in range(wx):
        plane_in(x).start()
    edge = 8
    for j, k in enumerate(EAST):
        held[k, 0] = from_w[j]
    for j, k in enumerate(WEST):
        held[k, wx + 1] = from_e[j]
    for ids, src, at in ((NORTH, from_s, 0), (SOUTH, from_n, 5)):
        for j, k in enumerate(ids):
            rows[at + j, edge : edge + wx, :] = src[j]
            if k in CORNERS:
                n = CORNERS.index(k)
                if lattice_dirs[k][0] == 1:
                    rows[at + j, edge - 1 : edge, :] = from_c[n, wx - 1 : wx, :]
                else:
                    rows[at + j, edge + wx : edge + wx + 1, :] = from_c[n, 0:1, :]
    plane_in(0).wait()
    row_at = iota((wy, nz), 0)
    lane_at = iota((wy, nz), 1)

    def one_plane(x, carry):
        @pl.when(x < wx - 1)
        def _():
            plane_in(x + 1).wait()

        for i in range(NDIR):
            sx, sy, sz = lattice_dirs[i]
            val = held[i, x + 1 - sx]
            if sy:
                line = (NORTH.index(i)) if sy == 1 else 5 + SOUTH.index(i)
                fill = rows[line, pl.ds(edge + x - sx, 1), :]
                val = pltpu.roll(val, sy % wy, 0)
                val = jnp.where(row_at == (0 if sy == 1 else wy - 1), fill, val)
            if sz:
                val = pltpu.roll(val, sz % nz, 1)
                mirror = held[opposite_dir[i], x + 1]
                val = jnp.where(lane_at == (0 if sz == 1 else nz - 1), mirror, val)
            outs[i, x] = val

        @pl.when(x > 0)
        def _():
            plane_out(x - 1).start()

        return carry

    lax.fori_loop(0, wx, one_plane, 0)
    plane_out(wx - 1).start()
    for x in range(wx):
        plane_out(x).wait()


def unsort_kernel(turbines, turb_ref, rank_ref, pfs_ref, out_ref):
    group = pfs_ref.shape[1]
    points = turb_ref.shape[1]
    data = jnp.concatenate(split3(pfs_ref[...]), axis=0).astype(bf16)
    n = 3 * turbines

    def chunk(k, carry):
        cols = pl.ds(pl.multiple_of(k * SORT_CHUNK, SORT_CHUNK), SORT_CHUNK)
        mine = turb_ref[:, cols] == iota((turbines, SORT_CHUNK), 0)
        place = (rank_ref[:, cols] == iota((group, SORT_CHUNK), 0).astype(f32)).astype(f32)
        got = jnp.dot(data, place.astype(bf16), preferred_element_type=f32)
        got = got[:n] + got[n : 2 * n] + got[2 * n :]
        for c in range(3):
            out_ref[c : c + 1, cols] = jnp.sum(
                jnp.where(mine, got[c * turbines : (c + 1) * turbines], 0.0), axis=0, keepdims=True
            )
        return carry

    lax.fori_loop(0, points // SORT_CHUNK, chunk, 0)


def body(populations, solid_flags, point_cells, point_turbine, blade_speed, chord, turbine_gain):
    wx, wy, nz = populations.shape[1:]
    nx, ny = lax.axis_size("gx"), lax.axis_size("gy")
    turbines = turbine_gain.shape[0]
    points = point_turbine.shape[0]
    group = points // turbines
    vmem = pl.BlockSpec(memory_space=pltpu.VMEM)
    smem = pl.BlockSpec(memory_space=pltpu.SMEM)
    hbm = pl.BlockSpec(memory_space=pl.ANY)
    shape = jax.ShapeDtypeStruct
    params = pltpu.CompilerParams(vmem_limit_bytes=VLIM)
    onehot = point_turbine[None, :] == jnp.arange(turbines, dtype=jnp.int32)[:, None]
    hubs = jnp.max(jnp.where(onehot, point_cells[0][None, :], 0), axis=1)
    turb = point_turbine.reshape(1, points)
    dma = pltpu.SemaphoreType.DMA
    per = -(-3 * turbines // (8 * nx)) * 8

    samples, table, rank = pl.pallas_call(
        functools.partial(sample_kernel, turbines),
        out_shape=(
            shape((nx, per, group), f32),
            shape((6 * turbines, group), f32),
            shape((1, points), f32),
        ),
        in_specs=[smem, vmem, vmem, vmem, vmem, vmem, hbm],
        out_specs=(vmem, vmem, vmem),
        scratch_shapes=[
            pltpu.VMEM(populations.shape, f32),
            pltpu.VMEM((15 * turbines, group), f32),
            dma((wx,)),
        ],
        compiler_params=params,
        name="sample",
    )(
        hubs,
        point_cells,
        turb,
        blade_speed,
        chord.reshape(1, points),
        turbine_gain.reshape(turbines, 1),
        populations,
    )

    summed = pl.pallas_call(
        functools.partial(reduce_kernel, nx, ny),
        out_shape=shape((nx, per, group), f32),
        in_specs=[vmem],
        out_specs=vmem,
        scratch_shapes=[
            pltpu.VMEM((nx, per, group), f32),
            pltpu.VMEM((ny, per, group), f32),
            pltpu.VMEM((per, group), f32),
            dma((nx,)),
            dma((nx,)),
            dma((ny,)),
            dma((ny,)),
            dma((nx,)),
            dma((nx,)),
        ],
        compiler_params=pltpu.CompilerParams(collective_id=0, has_side_effects=True),
        name="reduce",
    )(samples)

    pfs, north, south, post = pl.pallas_call(
        functools.partial(collide_kernel, turbines, wx * nx, wy * ny),
        out_shape=(
            shape((3 * turbines, group), f32),
            shape((5, wx, nz), f32),
            shape((5, wx, nz), f32),
            shape(populations.shape, f32),
        ),
        in_specs=[smem, vmem, vmem, hbm, hbm],
        out_specs=(vmem, vmem, vmem, hbm),
        scratch_shapes=[
            pltpu.VMEM(populations.shape, f32),
            pltpu.VMEM((wx, wy, nz), jnp.int32),
            pltpu.VMEM((3, wx, wy, nz), f32),
            pltpu.VMEM((3 * wy, nz), f32),
            dma((wx + 1,)),
            dma((wx,)),
        ],
        compiler_params=params,
        name="collide",
    )(hubs, summed.reshape(nx * per, group), table, solid_flags, populations)

    halos = pl.pallas_call(
        functools.partial(halo_kernel, nx, ny, wx),
        out_shape=(
            shape((5, wy, nz), f32),
            shape((5, wy, nz), f32),
            shape((5, wx, nz), f32),
            shape((5, wx, nz), f32),
            shape((4, wx, nz), f32),
        ),
        in_specs=[hbm, vmem, vmem],
        out_specs=(vmem,) * 5,
        scratch_shapes=[dma((16,)), dma((16,))],
        compiler_params=pltpu.CompilerParams(collective_id=1, has_side_effects=True),
        name="halo",
    )(post, north, south)

    out = pl.pallas_call(
        stream_kernel,
        out_shape=shape(populations.shape, f32),
        in_specs=[hbm] + [vmem] * 5,
        out_specs=hbm,
        scratch_shapes=[
            pltpu.VMEM((NDIR, wx + 2, wy, nz), f32),
            pltpu.VMEM((10, wx + 16, nz), f32),
            pltpu.VMEM(populations.shape, f32),
            dma((wx,)),
            dma((wx,)),
        ],
        compiler_params=params,
        name="stream",
    )(post, *halos)

    point_force = pl.pallas_call(
        functools.partial(unsort_kernel, turbines),
        out_shape=shape((3, points), f32),
        in_specs=[vmem, vmem, vmem],
        out_specs=vmem,
        compiler_params=params,
        name="unsort",
    )(turb, rank, pfs)
    return out, point_force


def solution(mesh):
    in_specs = (P(None, "gx", "gy", None), P("gx", "gy", None), P(), P(), P(), P(), P())
    out_specs = (P(None, "gx", "gy", None), P())
    return jax.shard_map(body, mesh=mesh, in_specs=in_specs, out_specs=out_specs, check_vma=False)
```

```python
import functools
import math

import jax
import jax.numpy as jnp
import numpy as np
from jax import lax
from jax.experimental import pallas as pl
from jax.experimental.pallas import tpu as pltpu
from jax.sharding import PartitionSpec as P

SMEAR = 3
lattice_dirs = [
    (0, 0, 0),
    (1, 0, 0),
    (-1, 0, 0),
    (0, 1, 0),
    (0, -1, 0),
    (0, 0, 1),
    (0, 0, -1),
    (1, 1, 0),
    (-1, -1, 0),
    (1, -1, 0),
    (-1, 1, 0),
    (1, 0, 1),
    (-1, 0, -1),
    (1, 0, -1),
    (-1, 0, 1),
    (0, 1, 1),
    (0, -1, -1),
    (0, 1, -1),
    (0, -1, 1),
]
opposite_dir = [0, 2, 1, 4, 3, 6, 5, 8, 7, 10, 9, 12, 11, 14, 13, 16, 15, 18, 17]
lattice_wts = [1.0 / 3.0] + [1.0 / 18.0] * 6 + [1.0 / 36.0] * 12
relax_time = 0.8
kernel_scale = 1.5
NDIR = 19
EAST = [k for k in range(NDIR) if lattice_dirs[k][0] == 1]
WEST = [k for k in range(NDIR) if lattice_dirs[k][0] == -1]
NORTH = [k for k in range(NDIR) if lattice_dirs[k][1] == 1]
SOUTH = [k for k in range(NDIR) if lattice_dirs[k][1] == -1]
CORNERS = [7, 8, 9, 10]
MESH = pl.DeviceIdType.MESH
f32 = jnp.float32
bf16 = jnp.bfloat16
NT = (((1,), (1,)), ((), ()))
VLIM = 67043328 - 0 * 1024
STREAM_VLIM = 67043328 - 0 * 1024
SORT_CHUNK = 512


def split3(x):
    a = x.astype(bf16).astype(f32)
    r = x - a
    b = r.astype(bf16).astype(f32)
    return a, b, r - b


def iota(shape, dim):
    return lax.broadcasted_iota(jnp.int32, shape, dim)


def moments(g):
    side = g[1]
    for k in range(2, 7):
        side = side + g[k]
    diag = g[7]
    for k in range(8, 19):
        diag = diag + g[k]
    rho = g[0] * (1.0 / 3.0) + side * (1.0 / 18.0) + diag * (1.0 / 36.0)
    mom = []
    for axis in range(3):
        first, rest = None, None
        for k in range(1, 19, 2):
            step = lattice_dirs[k][axis]
            if step == 0:
                continue
            diff = g[k] - g[k + 1] if step == 1 else g[k + 1] - g[k]
            if k < 7:
                first = diff if first is None else first + diff
            else:
                rest = diff if rest is None else rest + diff
        mom.append(first * (1.0 / 18.0) + rest * (1.0 / 36.0))
    return rho, mom


LANES = 128


def fold_sizes(rows, group):
    rest = group % LANES
    half = -(-rows // 16) * 8 if 0 < rest <= LANES // 2 else 0
    total = rows * (group // LANES) + (half or (rows if rest else 0))
    return rest, half, total


def folded(x):
    rows, group = x.shape
    rest, half, _ = fold_sizes(rows, group)
    blocks = [x[:, i * LANES : (i + 1) * LANES] for i in range(group // LANES)]
    if rest:
        tail = x[:, group - rest :]
        if half:
            low = jnp.zeros((2 * half - rows, rest), f32)
            second = jnp.concatenate([tail[half:], low], axis=0) if low.shape[0] else tail[half:]
            tail = jnp.concatenate([tail[:half], second], axis=1)
        width = tail.shape[1]
        if width < LANES:
            tail = jnp.concatenate([tail, jnp.zeros((tail.shape[0], LANES - width), f32)], axis=1)
        blocks.append(tail)
    return blocks


def unfolded(flat, rows, group):
    rest, half, _ = fold_sizes(rows, group)
    n = group // LANES
    blocks = [flat[i * rows : (i + 1) * rows] for i in range(n)]
    if rest:
        if half:
            tail = flat[n * rows : n * rows + half]
            second = tail[: rows - half, rest : 2 * rest]
            blocks.append(jnp.concatenate([tail[:, :rest], second], axis=0))
        else:
            blocks.append(flat[n * rows : (n + 1) * rows, :rest])
    return jnp.concatenate(blocks, axis=1)


def sample_kernel(
    turbines,
    gain_ref,
    pack_ref,
    pops_hbm,
    flat_hbm,
    table_ref,
    rank_ref,
    hubs_ref,
    pops,
    acc_ref,
    samp_ref,
    flat_ref,
    hub_ref,
    sems,
):
    wx, wy, nz = pops.shape[1:]
    points = pack_ref.shape[1]
    group = points // turbines
    start_x = lax.axis_index("gx") * wx
    start_y = lax.axis_index("gy") * wy

    def plane_copy(x):
        return pltpu.make_async_copy(pops_hbm.at[:, x], pops.at[:, x], sems.at[x])

    for x in range(wx):
        plane_copy(x).start()

    lanes = 128
    chunks = points // lanes
    hot = []
    hubs = jnp.zeros((turbines, lanes), f32)
    for k in range(chunks):
        own = pack_ref[0:1, k * lanes : (k + 1) * lanes]
        hot.append((own == iota((turbines, lanes), 0).astype(f32)).astype(f32))
        hubs = jnp.maximum(hubs, hot[k] * pack_ref[1:2, k * lanes : (k + 1) * lanes])
    hubs_ref[...] = jnp.broadcast_to(
        jnp.max(hubs, axis=1, keepdims=True), (turbines, lanes)
    ).astype(jnp.int32)
    hub_copy = pltpu.make_async_copy(hubs_ref, hub_ref, sems.at[wx])
    hub_copy.start()
    gain = jnp.zeros((turbines, 1), f32)
    for t in range(turbines):
        gain = jnp.where(iota((turbines, 1), 0) == t, gain_ref[t], gain)
    stacked = jnp.concatenate(hot, axis=0).astype(bf16)
    upto = (iota((lanes, lanes), 0) <= iota((lanes, lanes), 1)).astype(bf16)
    inside = jnp.dot(stacked, upto, preferred_element_type=f32)
    whole = jnp.dot(stacked, jnp.ones((lanes, lanes), bf16), preferred_element_type=f32)
    before = jnp.full((turbines, lanes), -1.0, f32)
    for k in range(chunks):
        rows = slice(k * turbines, (k + 1) * turbines)
        rank = jnp.sum(hot[k] * (inside[rows] + before), axis=0, keepdims=True)
        rank_ref[:, k * lanes : (k + 1) * lanes] = rank
        before = before + whole[rows]

    acc_ref[...] = jnp.zeros_like(acc_ref)

    def sort_chunk(k, carry):
        cols = pl.ds(pl.multiple_of(k * SORT_CHUNK, SORT_CHUNK), SORT_CHUNK)
        mine = pack_ref[0:1, cols] == iota((turbines, SORT_CHUNK), 0).astype(f32)
        pos_y = pack_ref[2:3, cols]
        pos_z = pack_ref[3:4, cols]
        y_high = pos_y.astype(bf16).astype(f32)
        rows = [y_high, pos_y - y_high, pos_z]
        for c in range(3):
            rows += list(split3(pack_ref[4 + c : 5 + c, cols]))
        rows += list(split3(pack_ref[7:8, cols] * gain))
        data = jnp.concatenate([jnp.where(mine, r, 0.0) for r in rows], axis=0).astype(bf16)
        place = (rank_ref[:, cols] == iota((group, SORT_CHUNK), 0).astype(f32)).astype(f32)
        acc_ref[...] += lax.dot_general(
            data, place.astype(bf16), NT, preferred_element_type=f32
        )
        return carry

    lax.fori_loop(0, points // SORT_CHUNK, sort_chunk, 0)

    def part(j):
        return acc_ref[j * turbines : (j + 1) * turbines]

    table_ref[0:turbines] = part(0) + part(1)
    table_ref[turbines : 2 * turbines] = part(2)
    for q in range(4):
        at = 3 + 3 * q
        table_ref[(2 + q) * turbines : (3 + q) * turbines] = part(at) + part(at + 1) + part(at + 2)

    samp_ref[...] = jnp.zeros_like(samp_ref)
    for x in range(wx):
        plane_copy(x).wait()
    hub_copy.wait()

    def one_turbine(t, carry):
        lx = hub_ref[t, 0] - start_x

        @pl.when((lx >= 0) & (lx < wx))
        def _():
            rho, mom = moments([pops[i, lx] for i in range(NDIR)])
            vel = jnp.concatenate([m / rho for m in mom], axis=0)
            split = jnp.concatenate(split3(vel), axis=0).astype(bf16)
            pos_y = table_ref[pl.ds(t, 1), :].astype(jnp.int32)
            pos_z = table_ref[pl.ds(turbines + t, 1), :].astype(jnp.int32)
            pick_z = (iota((nz, group), 0) == pos_z).astype(f32).astype(bf16)
            at_z = jnp.dot(split, pick_z, preferred_element_type=f32)
            n = 3 * wy
            at_z = at_z[:n] + at_z[n : 2 * n] + at_z[2 * n :]
            pick_y = iota((wy, group), 0) + start_y == pos_y
            for c in range(3):
                one = jnp.sum(
                    jnp.where(pick_y, at_z[c * wy : (c + 1) * wy], 0.0), axis=0, keepdims=True
                )
                samp_ref[pl.ds(c * turbines + t, 1), :] = one

        return carry

    lax.fori_loop(0, turbines, one_turbine, 0)
    blocks = folded(samp_ref[...])
    flat_ref[...] = jnp.zeros_like(flat_ref)
    at = 0
    for block in blocks:
        flat_ref[at : at + block.shape[0]] = block
        at += block.shape[0]
    out_copy = pltpu.make_async_copy(flat_ref, flat_hbm, sems.at[wx])
    out_copy.start()
    out_copy.wait()


def reduce_kernel(nx, ny, s_ref, out_ref, mine, rx, ry, red, ss1, sr1, ss2, sr2, ss3, sr3):
    gx = lax.axis_index("gx")
    gy = lax.axis_index("gy")
    xs = [lax.rem(gx + k, nx) for k in range(nx)]
    ys = [lax.rem(gy + k, ny) for k in range(ny)]
    barrier = pltpu.get_barrier_semaphore()
    for k in range(1, nx):
        pl.semaphore_signal(barrier, inc=1, device_id=(xs[k], gy), device_id_type=MESH)
    for k in range(1, ny):
        pl.semaphore_signal(barrier, inc=1, device_id=(gx, ys[k]), device_id_type=MESH)
    pl.semaphore_wait(barrier, nx + ny - 2)

    first = []
    for k in range(1, nx):
        first.append(
            pltpu.make_async_remote_copy(
                src_ref=s_ref.at[xs[k]],
                dst_ref=rx.at[k],
                send_sem=ss1.at[k],
                recv_sem=sr1.at[k],
                device_id=(xs[k], gy),
                device_id_type=MESH,
            )
        )
        first[-1].start()
    own = pltpu.make_async_copy(s_ref.at[gx], mine, sr1.at[0])
    own.start()
    own.wait()
    total = mine[...]
    for k in range(1, nx):
        first[k - 1].wait_recv()
        total = total + rx[k]
    red[...] = total

    second = []
    for k in range(1, ny):
        second.append(
            pltpu.make_async_remote_copy(
                src_ref=red,
                dst_ref=ry.at[k],
                send_sem=ss2.at[k],
                recv_sem=sr2.at[k],
                device_id=(gx, ys[k]),
                device_id_type=MESH,
            )
        )
        second[-1].start()
    for k in range(1, ny):
        second[k - 1].wait_recv()
        total = total + ry[k]
    mine[...] = total
    keep = pltpu.make_async_copy(mine, out_ref.at[gx], ss1.at[0])
    keep.start()
    third = []
    for k in range(1, nx):
        third.append(
            pltpu.make_async_remote_copy(
                src_ref=mine,
                dst_ref=out_ref.at[gx],
                send_sem=ss3.at[k],
                recv_sem=sr3.at[k],
                device_id=(xs[k], gy),
                device_id_type=MESH,
            )
        )
        third[-1].start()
    for copy in first + second:
        copy.wait_send()
    keep.wait()
    for copy in third:
        copy.wait()


def wrapped(offset, total):
    offset = jnp.where(offset >= total // 2, offset - total, offset)
    return jnp.where(offset < -(total // 2), offset + total, offset)


def kernel_value(offset):
    dist = offset.astype(f32)
    return jnp.where(
        jnp.abs(offset) <= SMEAR, jnp.exp(-((dist / kernel_scale) ** 2)), jnp.float32(0.0)
    )


def collide_kernel(
    turbines,
    total_x,
    total_y,
    flat_hbm,
    hubs_ref,
    table_ref,
    solid_hbm,
    pops_hbm,
    pfs_ref,
    north_ref,
    south_ref,
    post_hbm,
    pops,
    solid,
    force,
    field,
    flat,
    hub_ref,
    sems,
    out_sems,
):
    wx, wy, nz = pops.shape[1:]
    group = table_ref.shape[1]
    start_x = lax.axis_index("gx") * wx
    start_y = lax.axis_index("gy") * wy

    def plane_copy(x):
        return pltpu.make_async_copy(pops_hbm.at[:, x], pops.at[:, x], sems.at[x])

    def plane_out(x):
        return pltpu.make_async_copy(pops.at[:, x], post_hbm.at[:, x], out_sems.at[x])

    flat_copy = pltpu.make_async_copy(flat_hbm, flat, sems.at[wx + 1])
    flat_copy.start()
    hub_copy = pltpu.make_async_copy(hubs_ref, hub_ref, sems.at[wx + 2])
    hub_copy.start()
    solid_copy = pltpu.make_async_copy(solid_hbm, solid, sems.at[wx])
    solid_copy.start()
    for x in range(wx):
        plane_copy(x).start()

    def rows(j):
        return table_ref[j * turbines : (j + 1) * turbines]

    force[...] = jnp.zeros_like(force)
    flat_copy.wait()
    samp = unfolded(flat[...], 3 * turbines, group)
    rel = [samp[c * turbines : (c + 1) * turbines] - rows(2 + c) for c in range(3)]
    speed = jnp.sqrt(rel[0] * rel[0] + rel[1] * rel[1] + rel[2] * rel[2] + 0.0001)
    scale = -(rows(5) * speed)
    for c in range(3):
        pfs_ref[c * turbines : (c + 1) * turbines] = scale * rel[c]

    hub_copy.wait()
    reach = [float(np.float32(math.exp(-((d / kernel_scale) ** 2)))) for d in range(SMEAR + 1)]

    def one_turbine(t, carry):
        hub = hub_ref[t, 0]

        @pl.when(lax.rem(hub - start_x + SMEAR + total_x, total_x) < wx + 2 * SMEAR)
        def _():
            pos_y = table_ref[pl.ds(t, 1), :].astype(jnp.int32)
            pos_z = table_ref[pl.ds(turbines + t, 1), :].astype(jnp.int32)
            kern_y = kernel_value(wrapped(iota((wy, group), 0) + start_y - pos_y, total_y))
            kern_z = kernel_value(iota((nz, group), 0) - pos_z)
            left = jnp.concatenate(
                [kern_y * pfs_ref[pl.ds(c * turbines + t, 1), :] for c in range(3)], axis=0
            )
            field[...] = lax.dot_general(
                left, kern_z, NT, preferred_element_type=f32, precision=lax.Precision.HIGHEST
            )

            def one_plane(x, inner):
                away = jnp.abs(wrapped(start_x + x - hub, total_x))

                @pl.when(away <= SMEAR)
                def _():
                    kern_x = jnp.float32(reach[3])
                    for d in range(3):
                        kern_x = jnp.where(away == d, jnp.float32(reach[d]), kern_x)
                    for c in range(3):
                        force[c, x] += kern_x * field[c * wy : (c + 1) * wy]

                return inner

            lax.fori_loop(0, wx, one_plane, 0)

        return carry

    lax.fori_loop(0, turbines, one_turbine, 0)
    solid_copy.wait()
    step = 8

    def one_block(x, b):
        at = pl.ds(pl.multiple_of(b * step, step), step)
        g = [pops[i, x, at, :] for i in range(NDIR)]
        rho, mom = moments(g)
        frc = [force[c, x, at, :] for c in range(3)]
        inv = 1.0 / rho
        vel = [(mom[c] + 0.5 * frc[c]) * inv for c in range(3)]
        wall = solid[x, at, :] != 0
        usq = vel[0] * vel[0] + vel[1] * vel[1] + vel[2] * vel[2]
        uf = vel[0] * frc[0] + vel[1] * frc[1] + vel[2] * frc[2]
        om = 1.0 / relax_time
        pre = 1.0 - 0.5 / relax_time
        keep = 1.0 - om
        base = (om * rho) * (1.0 - 1.5 * usq) - (3.0 * pre) * uf
        quad = (4.5 * om) * rho
        lin = (3.0 * om) * rho
        pops[0, x, at, :] = jnp.where(wall, g[0], keep * g[0] + base)
        for k in range(1, NDIR, 2):
            cu, cf = None, None
            for axis in range(3):
                s = lattice_dirs[k][axis]
                if s == 0:
                    continue
                if cu is None:
                    cu, cf = (vel[axis], frc[axis]) if s == 1 else (-vel[axis], -frc[axis])
                elif s == 1:
                    cu, cf = cu + vel[axis], cf + frc[axis]
                else:
                    cu, cf = cu - vel[axis], cf - frc[axis]
            even = base + cu * (quad * cu + (9.0 * pre) * cf)
            odd = lin * cu + (3.0 * pre) * cf
            pops[k, x, at, :] = jnp.where(wall, g[k + 1], keep * g[k] + (even + odd))
            pops[k + 1, x, at, :] = jnp.where(wall, g[k], keep * g[k + 1] + (even - odd))

    def one_plane(x, carry):
        plane_copy(x).wait()

        def blocks(b, inner):
            one_block(x, b)
            return inner

        lax.fori_loop(0, wy // step, blocks, 0)
        for j, k in enumerate(NORTH):
            north_ref[j, pl.ds(x, 1), :] = pops[k, x, wy - 1 : wy, :]
        for j, k in enumerate(SOUTH):
            south_ref[j, pl.ds(x, 1), :] = pops[k, x, 0:1, :]

        @pl.when(x > 0)
        def _():
            plane_out(x - 1).start()

        return carry

    lax.fori_loop(0, wx, one_plane, 0)
    plane_out(wx - 1).start()
    for x in range(wx):
        plane_out(x).wait()


def halo_kernel(
    nx, ny, wx, post, north, south, from_w, from_e, from_s, from_n, from_c, send, recv
):
    gx = lax.axis_index("gx")
    gy = lax.axis_index("gy")
    east, west = lax.rem(gx + 1, nx), lax.rem(gx + nx - 1, nx)
    up, down = lax.rem(gy + 1, ny), lax.rem(gy + ny - 1, ny)
    barrier = pltpu.get_barrier_semaphore()
    near = [
        (east, gy), (west, gy), (gx, up), (gx, down),
        (east, up), (west, down), (east, down), (west, up),
    ]
    for dev in near:
        pl.semaphore_signal(barrier, inc=1, device_id=dev, device_id_type=MESH)
    pl.semaphore_wait(barrier, len(near))
    moves = []
    for j, k in enumerate(EAST):
        moves.append((post.at[k, wx - 1], from_w.at[j], (east, gy)))
    for j, k in enumerate(WEST):
        moves.append((post.at[k, 0], from_e.at[j], (west, gy)))
    moves.append((north, from_s, (gx, up)))
    moves.append((south, from_n, (gx, down)))
    for j, k in enumerate(CORNERS):
        side = north if k in NORTH else south
        ids = NORTH if k in NORTH else SOUTH
        moves.append((side.at[ids.index(k)], from_c.at[j], near[4 + j]))
    copies = []
    for n, (src, dst, dev) in enumerate(moves):
        copies.append(
            pltpu.make_async_remote_copy(
                src_ref=src,
                dst_ref=dst,
                send_sem=send.at[n],
                recv_sem=recv.at[n],
                device_id=dev,
                device_id_type=MESH,
            )
        )
        copies[-1].start()
    for copy in copies:
        copy.wait()


def stream_kernel(
    turbines,
    pack_ref,
    rank_ref,
    pfs_ref,
    post_hbm,
    from_w,
    from_e,
    from_s,
    from_n,
    from_c,
    out_hbm,
    pf_ref,
    held,
    rows,
    sides,
    corners,
    outs,
    sems,
    edge_sems,
    out_sems,
):
    wx = post_hbm.shape[1]
    wy, nz = post_hbm.shape[2:]

    def plane_in(x):
        return pltpu.make_async_copy(post_hbm.at[:, x], held.at[:, x + 1], sems.at[x])

    def plane_out(x):
        return pltpu.make_async_copy(outs.at[:, x], out_hbm.at[:, x], out_sems.at[x])

    for x in range(wx):
        plane_in(x).start()
    edge = 8
    edges = []
    for j, k in enumerate(EAST):
        edges.append((from_w.at[j], held.at[k, 0]))
    for j, k in enumerate(WEST):
        edges.append((from_e.at[j], held.at[k, wx + 1]))
    edges += [(from_s, sides.at[0]), (from_n, sides.at[1]), (from_c, corners)]
    edges = [
        pltpu.make_async_copy(src, dst, edge_sems.at[n]) for n, (src, dst) in enumerate(edges)
    ]
    for copy in edges:
        copy.start()

    group = pfs_ref.shape[1]
    data = jnp.concatenate(split3(pfs_ref[...]), axis=0).astype(bf16)
    n_rows = 3 * turbines

    def chunk(k, carry):
        cols = pl.ds(pl.multiple_of(k * SORT_CHUNK, SORT_CHUNK), SORT_CHUNK)
        mine = pack_ref[0:1, cols] == iota((turbines, SORT_CHUNK), 0).astype(f32)
        place = (rank_ref[:, cols] == iota((group, SORT_CHUNK), 0).astype(f32)).astype(f32)
        got = jnp.dot(data, place.astype(bf16), preferred_element_type=f32)
        got = got[:n_rows] + got[n_rows : 2 * n_rows] + got[2 * n_rows :]
        for c in range(3):
            pf_ref[c : c + 1, cols] = jnp.sum(
                jnp.where(mine, got[c * turbines : (c + 1) * turbines], 0.0), axis=0, keepdims=True
            )
        return carry

    lax.fori_loop(0, pack_ref.shape[1] // SORT_CHUNK, chunk, 0)

    for copy in edges:
        copy.wait()
    for ids, side, at in ((NORTH, 0, 0), (SOUTH, 1, 5)):
        for j, k in enumerate(ids):
            rows[at + j, edge : edge + wx, :] = sides[side, j]
            if k in CORNERS:
                n = CORNERS.index(k)
                if lattice_dirs[k][0] == 1:
                    rows[at + j, edge - 1 : edge, :] = corners[n, wx - 1 : wx, :]
                else:
                    rows[at + j, edge + wx : edge + wx + 1, :] = corners[n, 0:1, :]
    plane_in(0).wait()
    row_at = iota((wy, nz), 0)
    lane_at = iota((wy, nz), 1)

    def one_plane(x, carry):
        @pl.when(x < wx - 1)
        def _():
            plane_in(x + 1).wait()

        for i in range(NDIR):
            sx, sy, sz = lattice_dirs[i]
            val = held[i, x + 1 - sx]
            if sy:
                line = (NORTH.index(i)) if sy == 1 else 5 + SOUTH.index(i)
                fill = rows[line, pl.ds(edge + x - sx, 1), :]
                val = pltpu.roll(val, sy % wy, 0)
                val = jnp.where(row_at == (0 if sy == 1 else wy - 1), fill, val)
            if sz:
                val = pltpu.roll(val, sz % nz, 1)
                mirror = held[opposite_dir[i], x + 1]
                val = jnp.where(lane_at == (0 if sz == 1 else nz - 1), mirror, val)
            outs[i, x] = val

        @pl.when(x > 0)
        def _():
            plane_out(x - 1).start()

        return carry

    lax.fori_loop(0, wx, one_plane, 0)
    plane_out(wx - 1).start()
    for x in range(wx):
        plane_out(x).wait()


def body(populations, solid_flags, point_cells, point_turbine, blade_speed, chord, turbine_gain):
    wx, wy, nz = populations.shape[1:]
    nx, ny = lax.axis_size("gx"), lax.axis_size("gy")
    turbines = turbine_gain.shape[0]
    points = point_turbine.shape[0]
    group = points // turbines
    vmem = pl.BlockSpec(memory_space=pltpu.VMEM)
    smem = pl.BlockSpec(memory_space=pltpu.SMEM)
    hbm = pl.BlockSpec(memory_space=pltpu.HBM)
    shape = jax.ShapeDtypeStruct
    params = pltpu.CompilerParams(vmem_limit_bytes=VLIM)
    dma = pltpu.SemaphoreType.DMA
    pack = jnp.stack(
        [point_turbine.astype(f32)]
        + [point_cells[d].astype(f32) for d in range(3)]
        + [blade_speed[d] for d in range(3)]
        + [chord]
    )
    flat_rows = fold_sizes(3 * turbines, group)[2]
    per = -(-flat_rows // (8 * nx)) * 8

    flat, table, rank, hubs = pl.pallas_call(
        functools.partial(sample_kernel, turbines),
        out_shape=(
            shape((nx * per, LANES), f32),
            shape((6 * turbines, group), f32),
            shape((1, points), f32),
            shape((turbines, LANES), jnp.int32),
        ),
        in_specs=[smem, vmem, hbm],
        out_specs=(hbm, vmem, vmem, vmem),
        scratch_shapes=[
            pltpu.VMEM(populations.shape, f32),
            pltpu.VMEM((15 * turbines, group), f32),
            pltpu.VMEM((3 * turbines, group), f32),
            pltpu.VMEM((nx * per, LANES), f32),
            pltpu.SMEM((turbines, LANES), jnp.int32),
            dma((wx + 1,)),
        ],
        compiler_params=params,
        name="sample",
    )(turbine_gain, pack, populations)

    summed = pl.pallas_call(
        functools.partial(reduce_kernel, nx, ny),
        out_shape=shape((nx, per, LANES), f32),
        in_specs=[hbm],
        out_specs=hbm,
        scratch_shapes=[
            pltpu.VMEM((per, LANES), f32),
            pltpu.VMEM((nx, per, LANES), f32),
            pltpu.VMEM((ny, per, LANES), f32),
            pltpu.VMEM((per, LANES), f32),
            dma((nx,)),
            dma((nx,)),
            dma((ny,)),
            dma((ny,)),
            dma((nx,)),
            dma((nx,)),
        ],
        compiler_params=pltpu.CompilerParams(collective_id=0, has_side_effects=True),
        name="reduce",
    )(flat.reshape(nx, per, LANES))

    pfs, north, south, post = pl.pallas_call(
        functools.partial(collide_kernel, turbines, wx * nx, wy * ny),
        out_shape=(
            shape((3 * turbines, group), f32),
            shape((5, wx, nz), f32),
            shape((5, wx, nz), f32),
            shape(populations.shape, f32),
        ),
        in_specs=[hbm, vmem, vmem, hbm, hbm],
        out_specs=(vmem, vmem, vmem, hbm),
        scratch_shapes=[
            pltpu.VMEM(populations.shape, f32),
            pltpu.VMEM((wx, wy, nz), jnp.int32),
            pltpu.VMEM((3, wx, wy, nz), f32),
            pltpu.VMEM((3 * wy, nz), f32),
            pltpu.VMEM((nx * per, LANES), f32),
            pltpu.SMEM((turbines, LANES), jnp.int32),
            dma((wx + 3,)),
            dma((wx,)),
        ],
        compiler_params=params,
        name="collide",
    )(summed.reshape(nx * per, LANES), hubs, table, solid_flags, populations)

    halos = pl.pallas_call(
        functools.partial(halo_kernel, nx, ny, wx),
        out_shape=(
            shape((5, wy, nz), f32),
            shape((5, wy, nz), f32),
            shape((5, wx, nz), f32),
            shape((5, wx, nz), f32),
            shape((4, wx, nz), f32),
        ),
        in_specs=[hbm, hbm, hbm],
        out_specs=(hbm,) * 5,
        scratch_shapes=[dma((16,)), dma((16,))],
        compiler_params=pltpu.CompilerParams(collective_id=1, has_side_effects=True),
        name="halo",
    )(post, north, south)

    return pl.pallas_call(
        functools.partial(stream_kernel, turbines),
        out_shape=(shape(populations.shape, f32), shape((3, points), f32)),
        in_specs=[vmem] * 3 + [hbm] * 6,
        out_specs=(hbm, vmem),
        scratch_shapes=[
            pltpu.VMEM((NDIR, wx + 2, wy, nz), f32),
            pltpu.VMEM((10, wx + 16, nz), f32),
            pltpu.VMEM((2, 5, wx, nz), f32),
            pltpu.VMEM((4, wx, nz), f32),
            pltpu.VMEM(populations.shape, f32),
            dma((wx,)),
            dma((13,)),
            dma((wx,)),
        ],
        compiler_params=pltpu.CompilerParams(vmem_limit_bytes=STREAM_VLIM),
        name="stream",
    )(pack, rank, pfs, post, *halos)


def solution(mesh):
    in_specs = (P(None, "gx", "gy", None), P("gx", "gy", None), P(), P(), P(), P(), P())
    out_specs = (P(None, "gx", "gy", None), P())
    return jax.shard_map(body, mesh=mesh, in_specs=in_specs, out_specs=out_specs, check_vma=False)
```

```python
import functools
import math

import jax
import jax.numpy as jnp
import numpy as np
from jax import lax
from jax.experimental import pallas as pl
from jax.experimental.pallas import tpu as pltpu
from jax.sharding import PartitionSpec as P

SMEAR = 3
lattice_dirs = [
    (0, 0, 0),
    (1, 0, 0),
    (-1, 0, 0),
    (0, 1, 0),
    (0, -1, 0),
    (0, 0, 1),
    (0, 0, -1),
    (1, 1, 0),
    (-1, -1, 0),
    (1, -1, 0),
    (-1, 1, 0),
    (1, 0, 1),
    (-1, 0, -1),
    (1, 0, -1),
    (-1, 0, 1),
    (0, 1, 1),
    (0, -1, -1),
    (0, 1, -1),
    (0, -1, 1),
]
opposite_dir = [0, 2, 1, 4, 3, 6, 5, 8, 7, 10, 9, 12, 11, 14, 13, 16, 15, 18, 17]
lattice_wts = [1.0 / 3.0] + [1.0 / 18.0] * 6 + [1.0 / 36.0] * 12
relax_time = 0.8
kernel_scale = 1.5
NDIR = 19
EAST = [k for k in range(NDIR) if lattice_dirs[k][0] == 1]
WEST = [k for k in range(NDIR) if lattice_dirs[k][0] == -1]
NORTH = [k for k in range(NDIR) if lattice_dirs[k][1] == 1]
SOUTH = [k for k in range(NDIR) if lattice_dirs[k][1] == -1]
CORNERS = [7, 8, 9, 10]
MESH = pl.DeviceIdType.MESH
f32 = jnp.float32
bf16 = jnp.bfloat16
NT = (((1,), (1,)), ((), ()))
VLIM = 67043328 - 0 * 1024
STREAM_VLIM = 67043328 - 0 * 1024
SORT_CHUNK = 512


def split3(x):
    a = x.astype(bf16).astype(f32)
    r = x - a
    b = r.astype(bf16).astype(f32)
    return a, b, r - b


def iota(shape, dim):
    return lax.broadcasted_iota(jnp.int32, shape, dim)


def moments(g):
    side = g[1]
    for k in range(2, 7):
        side = side + g[k]
    diag = g[7]
    for k in range(8, 19):
        diag = diag + g[k]
    rho = g[0] * (1.0 / 3.0) + side * (1.0 / 18.0) + diag * (1.0 / 36.0)
    mom = []
    for axis in range(3):
        first, rest = None, None
        for k in range(1, 19, 2):
            step = lattice_dirs[k][axis]
            if step == 0:
                continue
            diff = g[k] - g[k + 1] if step == 1 else g[k + 1] - g[k]
            if k < 7:
                first = diff if first is None else first + diff
            else:
                rest = diff if rest is None else rest + diff
        mom.append(first * (1.0 / 18.0) + rest * (1.0 / 36.0))
    return rho, mom


LANES = 128


def fold_sizes(rows, group):
    rest = group % LANES
    half = -(-rows // 16) * 8 if 0 < rest <= LANES // 2 else 0
    total = rows * (group // LANES) + (half or (rows if rest else 0))
    return rest, half, total


def folded(x):
    rows, group = x.shape
    rest, half, _ = fold_sizes(rows, group)
    blocks = [x[:, i * LANES : (i + 1) * LANES] for i in range(group // LANES)]
    if rest:
        tail = x[:, group - rest :]
        if half:
            low = jnp.zeros((2 * half - rows, rest), f32)
            second = jnp.concatenate([tail[half:], low], axis=0) if low.shape[0] else tail[half:]
            tail = jnp.concatenate([tail[:half], second], axis=1)
        width = tail.shape[1]
        if width < LANES:
            tail = jnp.concatenate([tail, jnp.zeros((tail.shape[0], LANES - width), f32)], axis=1)
        blocks.append(tail)
    return blocks


def unfolded(flat, rows, group):
    rest, half, _ = fold_sizes(rows, group)
    n = group // LANES
    blocks = [flat[i * rows : (i + 1) * rows] for i in range(n)]
    if rest:
        if half:
            tail = flat[n * rows : n * rows + half]
            second = tail[: rows - half, rest : 2 * rest]
            blocks.append(jnp.concatenate([tail[:, :rest], second], axis=0))
        else:
            blocks.append(flat[n * rows : (n + 1) * rows, :rest])
    return jnp.concatenate(blocks, axis=1)


def sample_kernel(
    turbines,
    gain_ref,
    cells_ref,
    turb_ref,
    blade_ref,
    chord_ref,
    pops_hbm,
    flat_hbm,
    table_ref,
    rank_ref,
    hubs_ref,
    pops,
    acc_ref,
    samp_ref,
    flat_ref,
    hub_ref,
    pack_ref,
    sems,
):
    wx, wy, nz = pops.shape[1:]
    points = pack_ref.shape[1]
    group = points // turbines
    start_x = lax.axis_index("gx") * wx
    start_y = lax.axis_index("gy") * wy

    def plane_copy(x):
        return pltpu.make_async_copy(pops_hbm.at[:, x], pops.at[:, x], sems.at[x])

    for x in range(wx):
        plane_copy(x).start()

    for k in range(points // LANES):
        cols = slice(k * LANES, (k + 1) * LANES)
        turb = turb_ref[cols].astype(f32).reshape(1, LANES)
        pack_ref[0:1, cols] = turb
        rank_ref[1:2, cols] = turb
        pack_ref[7:8, cols] = chord_ref[cols].reshape(1, LANES)
    pack_ref[1:4, :] = cells_ref[...].astype(f32)
    pack_ref[4:7, :] = blade_ref[...]

    lanes = 128
    chunks = points // lanes
    hot = []
    hubs = jnp.zeros((turbines, lanes), f32)
    for k in range(chunks):
        own = pack_ref[0:1, k * lanes : (k + 1) * lanes]
        hot.append((own == iota((turbines, lanes), 0).astype(f32)).astype(f32))
        hubs = jnp.maximum(hubs, hot[k] * pack_ref[1:2, k * lanes : (k + 1) * lanes])
    hubs_ref[...] = jnp.broadcast_to(
        jnp.max(hubs, axis=1, keepdims=True), (turbines, lanes)
    ).astype(jnp.int32)
    hub_copy = pltpu.make_async_copy(hubs_ref, hub_ref, sems.at[wx])
    hub_copy.start()
    gain = jnp.zeros((turbines, 1), f32)
    for t in range(turbines):
        gain = jnp.where(iota((turbines, 1), 0) == t, gain_ref[t], gain)
    stacked = jnp.concatenate(hot, axis=0).astype(bf16)
    upto = (iota((lanes, lanes), 0) <= iota((lanes, lanes), 1)).astype(bf16)
    inside = jnp.dot(stacked, upto, preferred_element_type=f32)
    whole = jnp.dot(stacked, jnp.ones((lanes, lanes), bf16), preferred_element_type=f32)
    before = jnp.full((turbines, lanes), -1.0, f32)
    for k in range(chunks):
        rows = slice(k * turbines, (k + 1) * turbines)
        rank = jnp.sum(hot[k] * (inside[rows] + before), axis=0, keepdims=True)
        rank_ref[0:1, k * lanes : (k + 1) * lanes] = rank
        before = before + whole[rows]

    acc_ref[...] = jnp.zeros_like(acc_ref)

    def sort_chunk(k, carry):
        cols = pl.ds(pl.multiple_of(k * SORT_CHUNK, SORT_CHUNK), SORT_CHUNK)
        mine = pack_ref[0:1, cols] == iota((turbines, SORT_CHUNK), 0).astype(f32)
        pos_y = pack_ref[2:3, cols]
        pos_z = pack_ref[3:4, cols]
        y_high = pos_y.astype(bf16).astype(f32)
        rows = [y_high, pos_y - y_high, pos_z]
        for c in range(3):
            rows += list(split3(pack_ref[4 + c : 5 + c, cols]))
        rows += list(split3(pack_ref[7:8, cols] * gain))
        data = jnp.concatenate([jnp.where(mine, r, 0.0) for r in rows], axis=0).astype(bf16)
        place = (rank_ref[0:1, cols] == iota((group, SORT_CHUNK), 0).astype(f32)).astype(f32)
        acc_ref[...] += lax.dot_general(
            data, place.astype(bf16), NT, preferred_element_type=f32
        )
        return carry

    lax.fori_loop(0, points // SORT_CHUNK, sort_chunk, 0)

    def part(j):
        return acc_ref[j * turbines : (j + 1) * turbines]

    table_ref[0:turbines] = part(0) + part(1)
    table_ref[turbines : 2 * turbines] = part(2)
    for q in range(4):
        at = 3 + 3 * q
        table_ref[(2 + q) * turbines : (3 + q) * turbines] = part(at) + part(at + 1) + part(at + 2)

    samp_ref[...] = jnp.zeros_like(samp_ref)
    for x in range(wx):
        plane_copy(x).wait()
    hub_copy.wait()

    def one_turbine(t, carry):
        lx = hub_ref[t, 0] - start_x

        @pl.when((lx >= 0) & (lx < wx))
        def _():
            rho, mom = moments([pops[i, lx] for i in range(NDIR)])
            vel = jnp.concatenate([m / rho for m in mom], axis=0)
            split = jnp.concatenate(split3(vel), axis=0).astype(bf16)
            pos_y = table_ref[pl.ds(t, 1), :].astype(jnp.int32)
            pos_z = table_ref[pl.ds(turbines + t, 1), :].astype(jnp.int32)
            pick_z = (iota((nz, group), 0) == pos_z).astype(f32).astype(bf16)
            at_z = jnp.dot(split, pick_z, preferred_element_type=f32)
            n = 3 * wy
            at_z = at_z[:n] + at_z[n : 2 * n] + at_z[2 * n :]
            pick_y = iota((wy, group), 0) + start_y == pos_y
            for c in range(3):
                one = jnp.sum(
                    jnp.where(pick_y, at_z[c * wy : (c + 1) * wy], 0.0), axis=0, keepdims=True
                )
                samp_ref[pl.ds(c * turbines + t, 1), :] = one

        return carry

    lax.fori_loop(0, turbines, one_turbine, 0)
    blocks = folded(samp_ref[...])
    flat_ref[...] = jnp.zeros_like(flat_ref)
    at = 0
    for block in blocks:
        flat_ref[at : at + block.shape[0]] = block
        at += block.shape[0]
    out_copy = pltpu.make_async_copy(flat_ref, flat_hbm, sems.at[wx])
    out_copy.start()
    out_copy.wait()


def reduce_kernel(nx, ny, s_ref, out_ref, mine, rx, ry, red, ss1, sr1, ss2, sr2, ss3, sr3):
    gx = lax.axis_index("gx")
    gy = lax.axis_index("gy")
    xs = [lax.rem(gx + k, nx) for k in range(nx)]
    ys = [lax.rem(gy + k, ny) for k in range(ny)]
    barrier = pltpu.get_barrier_semaphore()
    for k in range(1, nx):
        pl.semaphore_signal(barrier, inc=1, device_id=(xs[k], gy), device_id_type=MESH)
    for k in range(1, ny):
        pl.semaphore_signal(barrier, inc=1, device_id=(gx, ys[k]), device_id_type=MESH)
    pl.semaphore_wait(barrier, nx + ny - 2)

    first = []
    for k in range(1, nx):
        first.append(
            pltpu.make_async_remote_copy(
                src_ref=s_ref.at[xs[k]],
                dst_ref=rx.at[k],
                send_sem=ss1.at[k],
                recv_sem=sr1.at[k],
                device_id=(xs[k], gy),
                device_id_type=MESH,
            )
        )
        first[-1].start()
    own = pltpu.make_async_copy(s_ref.at[gx], mine, sr1.at[0])
    own.start()
    own.wait()
    total = mine[...]
    for k in range(1, nx):
        first[k - 1].wait_recv()
        total = total + rx[k]
    red[...] = total

    second = []
    for k in range(1, ny):
        second.append(
            pltpu.make_async_remote_copy(
                src_ref=red,
                dst_ref=ry.at[k],
                send_sem=ss2.at[k],
                recv_sem=sr2.at[k],
                device_id=(gx, ys[k]),
                device_id_type=MESH,
            )
        )
        second[-1].start()
    for k in range(1, ny):
        second[k - 1].wait_recv()
        total = total + ry[k]
    mine[...] = total
    keep = pltpu.make_async_copy(mine, out_ref.at[gx], ss1.at[0])
    keep.start()
    third = []
    for k in range(1, nx):
        third.append(
            pltpu.make_async_remote_copy(
                src_ref=mine,
                dst_ref=out_ref.at[gx],
                send_sem=ss3.at[k],
                recv_sem=sr3.at[k],
                device_id=(xs[k], gy),
                device_id_type=MESH,
            )
        )
        third[-1].start()
    for copy in first + second:
        copy.wait_send()
    keep.wait()
    for copy in third:
        copy.wait()


def wrapped(offset, total):
    offset = jnp.where(offset >= total // 2, offset - total, offset)
    return jnp.where(offset < -(total // 2), offset + total, offset)


def kernel_value(offset):
    dist = offset.astype(f32)
    return jnp.where(
        jnp.abs(offset) <= SMEAR, jnp.exp(-((dist / kernel_scale) ** 2)), jnp.float32(0.0)
    )


def collide_kernel(
    turbines,
    total_x,
    total_y,
    flat_hbm,
    hubs_ref,
    table_ref,
    solid_hbm,
    pops_hbm,
    pfs_ref,
    north_ref,
    south_ref,
    post_hbm,
    pops,
    solid,
    force,
    field,
    flat,
    hub_ref,
    sems,
    out_sems,
):
    wx, wy, nz = pops.shape[1:]
    group = table_ref.shape[1]
    start_x = lax.axis_index("gx") * wx
    start_y = lax.axis_index("gy") * wy

    def plane_copy(x):
        return pltpu.make_async_copy(pops_hbm.at[:, x], pops.at[:, x], sems.at[x])

    def plane_out(x):
        return pltpu.make_async_copy(pops.at[:, x], post_hbm.at[:, x], out_sems.at[x])

    flat_copy = pltpu.make_async_copy(flat_hbm, flat, sems.at[wx + 1])
    flat_copy.start()
    hub_copy = pltpu.make_async_copy(hubs_ref, hub_ref, sems.at[wx + 2])
    hub_copy.start()
    solid_copy = pltpu.make_async_copy(solid_hbm, solid, sems.at[wx])
    solid_copy.start()
    for x in range(wx):
        plane_copy(x).start()

    def rows(j):
        return table_ref[j * turbines : (j + 1) * turbines]

    force[...] = jnp.zeros_like(force)
    flat_copy.wait()
    samp = unfolded(flat[...], 3 * turbines, group)
    rel = [samp[c * turbines : (c + 1) * turbines] - rows(2 + c) for c in range(3)]
    speed = jnp.sqrt(rel[0] * rel[0] + rel[1] * rel[1] + rel[2] * rel[2] + 0.0001)
    scale = -(rows(5) * speed)
    for c in range(3):
        pfs_ref[c * turbines : (c + 1) * turbines] = scale * rel[c]

    hub_copy.wait()
    reach = [float(np.float32(math.exp(-((d / kernel_scale) ** 2)))) for d in range(SMEAR + 1)]

    def one_turbine(t, carry):
        hub = hub_ref[t, 0]

        @pl.when(lax.rem(hub - start_x + SMEAR + total_x, total_x) < wx + 2 * SMEAR)
        def _():
            pos_y = table_ref[pl.ds(t, 1), :].astype(jnp.int32)
            pos_z = table_ref[pl.ds(turbines + t, 1), :].astype(jnp.int32)
            kern_y = kernel_value(wrapped(iota((wy, group), 0) + start_y - pos_y, total_y))
            kern_z = kernel_value(iota((nz, group), 0) - pos_z)
            left = jnp.concatenate(
                [kern_y * pfs_ref[pl.ds(c * turbines + t, 1), :] for c in range(3)], axis=0
            )
            field[...] = lax.dot_general(
                left, kern_z, NT, preferred_element_type=f32, precision=lax.Precision.HIGHEST
            )

            def one_plane(x, inner):
                away = jnp.abs(wrapped(start_x + x - hub, total_x))

                @pl.when(away <= SMEAR)
                def _():
                    kern_x = jnp.float32(reach[3])
                    for d in range(3):
                        kern_x = jnp.where(away == d, jnp.float32(reach[d]), kern_x)
                    for c in range(3):
                        force[c, x] += kern_x * field[c * wy : (c + 1) * wy]

                return inner

            lax.fori_loop(0, wx, one_plane, 0)

        return carry

    lax.fori_loop(0, turbines, one_turbine, 0)
    solid_copy.wait()
    step = 8

    def one_block(x, b):
        at = pl.ds(pl.multiple_of(b * step, step), step)
        g = [pops[i, x, at, :] for i in range(NDIR)]
        rho, mom = moments(g)
        frc = [force[c, x, at, :] for c in range(3)]
        inv = 1.0 / rho
        vel = [(mom[c] + 0.5 * frc[c]) * inv for c in range(3)]
        wall = solid[x, at, :] != 0
        usq = vel[0] * vel[0] + vel[1] * vel[1] + vel[2] * vel[2]
        uf = vel[0] * frc[0] + vel[1] * frc[1] + vel[2] * frc[2]
        om = 1.0 / relax_time
        pre = 1.0 - 0.5 / relax_time
        keep = 1.0 - om
        base = (om * rho) * (1.0 - 1.5 * usq) - (3.0 * pre) * uf
        quad = (4.5 * om) * rho
        lin = (3.0 * om) * rho
        pops[0, x, at, :] = jnp.where(wall, g[0], keep * g[0] + base)
        for k in range(1, NDIR, 2):
            cu, cf = None, None
            for axis in range(3):
                s = lattice_dirs[k][axis]
                if s == 0:
                    continue
                if cu is None:
                    cu, cf = (vel[axis], frc[axis]) if s == 1 else (-vel[axis], -frc[axis])
                elif s == 1:
                    cu, cf = cu + vel[axis], cf + frc[axis]
                else:
                    cu, cf = cu - vel[axis], cf - frc[axis]
            even = base + cu * (quad * cu + (9.0 * pre) * cf)
            odd = lin * cu + (3.0 * pre) * cf
            pops[k, x, at, :] = jnp.where(wall, g[k + 1], keep * g[k] + (even + odd))
            pops[k + 1, x, at, :] = jnp.where(wall, g[k], keep * g[k + 1] + (even - odd))

    def one_plane(x, carry):
        plane_copy(x).wait()

        def blocks(b, inner):
            one_block(x, b)
            return inner

        lax.fori_loop(0, wy // step, blocks, 0)
        for j, k in enumerate(NORTH):
            north_ref[j, pl.ds(x, 1), :] = pops[k, x, wy - 1 : wy, :]
        for j, k in enumerate(SOUTH):
            south_ref[j, pl.ds(x, 1), :] = pops[k, x, 0:1, :]

        @pl.when(x > 0)
        def _():
            plane_out(x - 1).start()

        return carry

    lax.fori_loop(0, wx, one_plane, 0)
    plane_out(wx - 1).start()
    for x in range(wx):
        plane_out(x).wait()


def halo_kernel(
    nx, ny, wx, post, north, south, from_w, from_e, from_s, from_n, from_c, send, recv
):
    gx = lax.axis_index("gx")
    gy = lax.axis_index("gy")
    east, west = lax.rem(gx + 1, nx), lax.rem(gx + nx - 1, nx)
    up, down = lax.rem(gy + 1, ny), lax.rem(gy + ny - 1, ny)
    barrier = pltpu.get_barrier_semaphore()
    near = [
        (east, gy), (west, gy), (gx, up), (gx, down),
        (east, up), (west, down), (east, down), (west, up),
    ]
    for dev in near:
        pl.semaphore_signal(barrier, inc=1, device_id=dev, device_id_type=MESH)
    pl.semaphore_wait(barrier, len(near))
    moves = []
    for j, k in enumerate(EAST):
        moves.append((post.at[k, wx - 1], from_w.at[j], (east, gy)))
    for j, k in enumerate(WEST):
        moves.append((post.at[k, 0], from_e.at[j], (west, gy)))
    moves.append((north, from_s, (gx, up)))
    moves.append((south, from_n, (gx, down)))
    for j, k in enumerate(CORNERS):
        side = north if k in NORTH else south
        ids = NORTH if k in NORTH else SOUTH
        moves.append((side.at[ids.index(k)], from_c.at[j], near[4 + j]))
    copies = []
    for n, (src, dst, dev) in enumerate(moves):
        copies.append(
            pltpu.make_async_remote_copy(
                src_ref=src,
                dst_ref=dst,
                send_sem=send.at[n],
                recv_sem=recv.at[n],
                device_id=dev,
                device_id_type=MESH,
            )
        )
        copies[-1].start()
    for copy in copies:
        copy.wait()


def stream_kernel(
    turbines,
    rank_ref,
    pfs_ref,
    post_hbm,
    from_w,
    from_e,
    from_s,
    from_n,
    from_c,
    out_hbm,
    pf_ref,
    held,
    rows,
    sides,
    corners,
    outs,
    sems,
    edge_sems,
    out_sems,
):
    wx = post_hbm.shape[1]
    wy, nz = post_hbm.shape[2:]

    def plane_in(x):
        return pltpu.make_async_copy(post_hbm.at[:, x], held.at[:, x + 1], sems.at[x])

    def plane_out(x):
        return pltpu.make_async_copy(outs.at[:, x], out_hbm.at[:, x], out_sems.at[x])

    for x in range(wx):
        plane_in(x).start()
    edge = 8
    edges = []
    for j, k in enumerate(EAST):
        edges.append((from_w.at[j], held.at[k, 0]))
    for j, k in enumerate(WEST):
        edges.append((from_e.at[j], held.at[k, wx + 1]))
    edges += [(from_s, sides.at[0]), (from_n, sides.at[1]), (from_c, corners)]
    edges = [
        pltpu.make_async_copy(src, dst, edge_sems.at[n]) for n, (src, dst) in enumerate(edges)
    ]
    for copy in edges:
        copy.start()

    group = pfs_ref.shape[1]
    data = jnp.concatenate(split3(pfs_ref[...]), axis=0).astype(bf16)
    n_rows = 3 * turbines

    def chunk(k, carry):
        cols = pl.ds(pl.multiple_of(k * SORT_CHUNK, SORT_CHUNK), SORT_CHUNK)
        mine = rank_ref[1:2, cols] == iota((turbines, SORT_CHUNK), 0).astype(f32)
        place = (rank_ref[0:1, cols] == iota((group, SORT_CHUNK), 0).astype(f32)).astype(f32)
        got = jnp.dot(data, place.astype(bf16), preferred_element_type=f32)
        got = got[:n_rows] + got[n_rows : 2 * n_rows] + got[2 * n_rows :]
        for c in range(3):
            pf_ref[c : c + 1, cols] = jnp.sum(
                jnp.where(mine, got[c * turbines : (c + 1) * turbines], 0.0), axis=0, keepdims=True
            )
        return carry

    lax.fori_loop(0, rank_ref.shape[1] // SORT_CHUNK, chunk, 0)

    for copy in edges:
        copy.wait()
    for ids, side, at in ((NORTH, 0, 0), (SOUTH, 1, 5)):
        for j, k in enumerate(ids):
            rows[at + j, edge : edge + wx, :] = sides[side, j]
            if k in CORNERS:
                n = CORNERS.index(k)
                if lattice_dirs[k][0] == 1:
                    rows[at + j, edge - 1 : edge, :] = corners[n, wx - 1 : wx, :]
                else:
                    rows[at + j, edge + wx : edge + wx + 1, :] = corners[n, 0:1, :]
    plane_in(0).wait()
    row_at = iota((wy, nz), 0)
    lane_at = iota((wy, nz), 1)

    def one_plane(x, carry):
        @pl.when(x < wx - 1)
        def _():
            plane_in(x + 1).wait()

        for i in range(NDIR):
            sx, sy, sz = lattice_dirs[i]
            val = held[i, x + 1 - sx]
            if sy:
                line = (NORTH.index(i)) if sy == 1 else 5 + SOUTH.index(i)
                fill = rows[line, pl.ds(edge + x - sx, 1), :]
                val = pltpu.roll(val, sy % wy, 0)
                val = jnp.where(row_at == (0 if sy == 1 else wy - 1), fill, val)
            if sz:
                val = pltpu.roll(val, sz % nz, 1)
                mirror = held[opposite_dir[i], x + 1]
                val = jnp.where(lane_at == (0 if sz == 1 else nz - 1), mirror, val)
            outs[i, x] = val

        @pl.when(x > 0)
        def _():
            plane_out(x - 1).start()

        return carry

    lax.fori_loop(0, wx, one_plane, 0)
    plane_out(wx - 1).start()
    for x in range(wx):
        plane_out(x).wait()


def body(populations, solid_flags, point_cells, point_turbine, blade_speed, chord, turbine_gain):
    wx, wy, nz = populations.shape[1:]
    nx, ny = lax.axis_size("gx"), lax.axis_size("gy")
    turbines = turbine_gain.shape[0]
    points = point_turbine.shape[0]
    group = points // turbines
    vmem = pl.BlockSpec(memory_space=pltpu.VMEM)
    smem = pl.BlockSpec(memory_space=pltpu.SMEM)
    hbm = pl.BlockSpec(memory_space=pltpu.HBM)
    shape = jax.ShapeDtypeStruct
    params = pltpu.CompilerParams(vmem_limit_bytes=VLIM)
    dma = pltpu.SemaphoreType.DMA
    flat_rows = fold_sizes(3 * turbines, group)[2]
    per = -(-flat_rows // (8 * nx)) * 8

    flat, table, rank, hubs = pl.pallas_call(
        functools.partial(sample_kernel, turbines),
        out_shape=(
            shape((nx * per, LANES), f32),
            shape((6 * turbines, group), f32),
            shape((2, points), f32),
            shape((turbines, LANES), jnp.int32),
        ),
        in_specs=[smem, vmem, vmem, vmem, vmem, hbm],
        out_specs=(hbm, vmem, vmem, vmem),
        scratch_shapes=[
            pltpu.VMEM(populations.shape, f32),
            pltpu.VMEM((15 * turbines, group), f32),
            pltpu.VMEM((3 * turbines, group), f32),
            pltpu.VMEM((nx * per, LANES), f32),
            pltpu.SMEM((turbines, LANES), jnp.int32),
            pltpu.VMEM((8, points), f32),
            dma((wx + 1,)),
        ],
        compiler_params=params,
        name="sample",
    )(turbine_gain, point_cells, point_turbine, blade_speed, chord, populations)

    summed = pl.pallas_call(
        functools.partial(reduce_kernel, nx, ny),
        out_shape=shape((nx, per, LANES), f32),
        in_specs=[hbm],
        out_specs=hbm,
        scratch_shapes=[
            pltpu.VMEM((per, LANES), f32),
            pltpu.VMEM((nx, per, LANES), f32),
            pltpu.VMEM((ny, per, LANES), f32),
            pltpu.VMEM((per, LANES), f32),
            dma((nx,)),
            dma((nx,)),
            dma((ny,)),
            dma((ny,)),
            dma((nx,)),
            dma((nx,)),
        ],
        compiler_params=pltpu.CompilerParams(collective_id=0, has_side_effects=True),
        name="reduce",
    )(flat.reshape(nx, per, LANES))

    pfs, north, south, post = pl.pallas_call(
        functools.partial(collide_kernel, turbines, wx * nx, wy * ny),
        out_shape=(
            shape((3 * turbines, group), f32),
            shape((5, wx, nz), f32),
            shape((5, wx, nz), f32),
            shape(populations.shape, f32),
        ),
        in_specs=[hbm, vmem, vmem, hbm, hbm],
        out_specs=(vmem, vmem, vmem, hbm),
        scratch_shapes=[
            pltpu.VMEM(populations.shape, f32),
            pltpu.VMEM((wx, wy, nz), jnp.int32),
            pltpu.VMEM((3, wx, wy, nz), f32),
            pltpu.VMEM((3 * wy, nz), f32),
            pltpu.VMEM((nx * per, LANES), f32),
            pltpu.SMEM((turbines, LANES), jnp.int32),
            dma((wx + 3,)),
            dma((wx,)),
        ],
        compiler_params=params,
        name="collide",
    )(summed.reshape(nx * per, LANES), hubs, table, solid_flags, populations)

    halos = pl.pallas_call(
        functools.partial(halo_kernel, nx, ny, wx),
        out_shape=(
            shape((5, wy, nz), f32),
            shape((5, wy, nz), f32),
            shape((5, wx, nz), f32),
            shape((5, wx, nz), f32),
            shape((4, wx, nz), f32),
        ),
        in_specs=[hbm, hbm, hbm],
        out_specs=(hbm,) * 5,
        scratch_shapes=[dma((16,)), dma((16,))],
        compiler_params=pltpu.CompilerParams(collective_id=1, has_side_effects=True),
        name="halo",
    )(post, north, south)

    return pl.pallas_call(
        functools.partial(stream_kernel, turbines),
        out_shape=(shape(populations.shape, f32), shape((3, points), f32)),
        in_specs=[vmem] * 2 + [hbm] * 6,
        out_specs=(hbm, vmem),
        scratch_shapes=[
            pltpu.VMEM((NDIR, wx + 2, wy, nz), f32),
            pltpu.VMEM((10, wx + 16, nz), f32),
            pltpu.VMEM((2, 5, wx, nz), f32),
            pltpu.VMEM((4, wx, nz), f32),
            pltpu.VMEM(populations.shape, f32),
            dma((wx,)),
            dma((13,)),
            dma((wx,)),
        ],
        compiler_params=pltpu.CompilerParams(vmem_limit_bytes=STREAM_VLIM),
        name="stream",
    )(rank, pfs, post, *halos)


def solution(mesh):
    in_specs = (P(None, "gx", "gy", None), P("gx", "gy", None), P(), P(), P(), P(), P())
    out_specs = (P(None, "gx", "gy", None), P())
    return jax.shard_map(body, mesh=mesh, in_specs=in_specs, out_specs=out_specs, check_vma=False)
```
